32 devices in a mesh: batch: 4 (over y, core), seq: 8 (over z, x).
Axes of the slice: x: 2, y: 2, z: 4, core: 2. Of those that a mesh axis runs over, the one named last changes fastest.
Arguments:
- tokens: bfloat16 [4, 1024, 1024], P('batch', 'seq'), may hold values from -6 to 6
- w_query: bfloat16 [512, 512], replicated, may hold values from -0.25 to 0.25
- w_value: bfloat16 [512, 512], replicated, may hold values from -0.25 to 0.25
- w_out: bfloat16 [512, 512], replicated, may hold values from -0.25 to 0.25
- long_filter: float32 [512, 1024], P('seq'), may hold values from -0.1875 to 0.1875
- cotangent: bfloat16 [4, 1024, 1024], P('batch', 'seq'), may hold values from -6 to 6
Outputs:
- block_out: bfloat16 [4, 1024, 1024], P('batch', 'seq')
- grad_tokens: bfloat16 [4, 1024, 1024], P('batch', 'seq')
- grad_query: float32 [512, 512], P('seq')
- grad_value: float32 [512, 512], P('seq')
- grad_out: float32 [512, 512], P('seq')
- grad_filter: float32 [512, 1024], P('seq')
The draws below stay inside these ranges and needn't reach their ends.
All inputs are finite; a program needn't handle non-finite values.
Results may differ from the reference program's by a relative error of at most 0.017.
Values may be sent and summed in bfloat16 or wider, within the bound.
A program may use at most 64 MiB of HBM per device.

```python
import jax
import jax.numpy as jnp

D = 1024
HALF = 512
LENGTH = 1024
SEQS = 4


def raised(entries, stream_key, source, target, shards_of, factor):
    owner, partner = [(jnp.arange(entries.shape[dim]) // (entries.shape[dim] // shards_of)).reshape([-1 if axis == dim else 1 for axis in range(entries.ndim)]) for dim in (source, target)]
    chosen = jax.random.permutation(stream_key, shards_of)[partner]
    strong = (owner == chosen) | (owner == (partner + shards_of // 2) % shards_of)
    return jnp.where(strong, factor * entries, entries)


def block_scale(own_key, dims, shards, smallest, top_value):
    gain = 1.0
    for position, shards_of in shards:
        draws = jax.random.uniform(jax.random.fold_in(jax.random.fold_in(own_key, 6), position), (shards_of,), jnp.float32, smallest / len(shards), top_value / len(shards))
        gain = gain * jnp.repeat(jnp.exp(draws), dims[position] // shards_of).reshape((-1,) + (1,) * (len(dims) - 1 - position))
    return gain


def gaussian(own_key, dims, scale, most, pieces=(), kind=jnp.bfloat16):
    level = block_scale(own_key, dims, pieces, -0.22, 0.18) if pieces else 1.0
    drawn = jax.random.normal(own_key, dims, jnp.float32) * scale * level
    return jnp.minimum(jnp.maximum(drawn, -most), most).astype(kind)


def noise_with(key, dims, deviation, limit, split, heavy, held_as=jnp.bfloat16):
    entries = deviation * jax.random.normal(key, dims, jnp.float32)
    if split:
        entries = entries * block_scale(key, dims, split, -0.22, 0.18)
    return jnp.clip(raised(entries, jax.random.fold_in(key, 3), *heavy), -limit, limit).astype(held_as)


def setup_inputs(seed: int = 0) -> dict:
    arg_keys = jax.random.split(jax.random.key(seed), 7)
    return {
        "tokens": noise_with(arg_keys[0], (SEQS, LENGTH, D), 1.0, 6.0, ((0, 4), (1, 8)), (1, 2, 8, 2.0)),
        "w_query": gaussian(arg_keys[1], (HALF, HALF), HALF ** -0.5, 0.25),
        "w_value": gaussian(arg_keys[2], (HALF, HALF), HALF ** -0.5, 0.25),
        "w_out": gaussian(arg_keys[3], (HALF, HALF), HALF ** -0.5, 0.25),
        "long_filter": gaussian(arg_keys[4], (HALF, LENGTH), LENGTH ** -0.5, 0.1875, ((0, 8),), jnp.float32),
        "cotangent": gaussian(arg_keys[5], (SEQS, LENGTH, D), 1.0, 6.0, ((0, 4), (1, 8))),
    }


def rc_flip(block):
    return block[::-1, ::-1]


def reference(tokens, w_query, w_value, w_out, long_filter, cotangent):
    floats = jnp.float32
    halves = jnp.bfloat16
    half = HALF
    length = LENGTH
    period = 2 * LENGTH
    scale = (2.0 * SEQS * LENGTH) ** -0.5
    taps = jnp.fft.fft(long_filter, n=period, axis=1)
    query_weight = w_query.astype(floats)
    value_weight = w_value.astype(floats)
    out_weight = w_out.astype(floats)
    total_query = jnp.zeros((half, half), floats)
    total_value = jnp.zeros((half, half), floats)
    total_out = jnp.zeros((half, half), floats)
    total_filter = jnp.zeros((half, length), floats)
    outputs = []
    gradients = []
    for sequence in range(SEQS):
        source = tokens[sequence]
        front = source[:, :half]
        back = source[:, half:]
        strands = jnp.stack([front, rc_flip(back)]).astype(floats)
        query = jnp.einsum('stk,kh->sht', strands, query_weight).astype(halves)
        value = jnp.einsum('stk,kh->sht', strands, value_weight).astype(halves)
        value_spec = jnp.fft.fft(value.astype(floats), n=period, axis=2)
        conv = jnp.fft.ifft(value_spec * taps[None], axis=2)[:, :, :length].real.astype(halves)
        gated = (query.astype(floats) * conv.astype(floats)).astype(halves)
        projected = jnp.einsum('sht,hk->stk', gated.astype(floats), out_weight)
        block = jnp.concatenate([front.astype(floats) + projected[0], back.astype(floats) + rc_flip(projected[1])], axis=1)
        outputs.append(block.astype(halves))
        upstream = cotangent[sequence]
        grad_strands = jnp.stack([upstream[:, :half], rc_flip(upstream[:, half:])]).astype(floats)
        grad_gated = jnp.einsum('stk,hk->sht', grad_strands, out_weight).astype(halves)
        grad_query_t = (grad_gated.astype(floats) * conv.astype(floats)).astype(halves)
        grad_conv = (grad_gated.astype(floats) * query.astype(floats)).astype(halves)
        grad_spec = jnp.fft.fft(grad_conv.astype(floats), n=period, axis=2)
        grad_value_t = jnp.fft.ifft(grad_spec * jnp.conj(taps)[None], axis=2)[:, :, :length].real.astype(halves)
        filter_spec = jnp.sum(jnp.conj(value_spec) * grad_spec, axis=0)
        total_filter = total_filter + jnp.fft.ifft(filter_spec, axis=1)[:, :length].real.astype(floats)
        input_grad = jnp.einsum('sht,kh->stk', grad_query_t.astype(floats), query_weight) + jnp.einsum('sht,kh->stk', grad_value_t.astype(floats), value_weight)
        grad_block = jnp.concatenate([upstream[:, :half].astype(floats) + input_grad[0], upstream[:, half:].astype(floats) + rc_flip(input_grad[1])], axis=1)
        gradients.append(grad_block.astype(halves))
        total_query = total_query + jnp.einsum('stk,sht->kh', strands, grad_query_t.astype(floats))
        total_value = total_value + jnp.einsum('stk,sht->kh', strands, grad_value_t.astype(floats))
        total_out = total_out + jnp.einsum('sht,stk->hk', gated.astype(floats), grad_strands)
    return (jnp.stack(outputs), jnp.stack(gradients), total_query * scale, total_value * scale, total_out * scale, total_filter * scale)
```

```python
import functools
import math

import jax
import jax.numpy as jnp
import numpy as np
from jax import lax
from jax.experimental import pallas as pl
from jax.experimental.pallas import tpu as pltpu
from jax.sharding import PartitionSpec as P

precise = lax.Precision.HIGH


def swapped(x, axis, stride):
    return lax.ppermute(x, axis, [(i, i ^ 1 << stride) for i in range(lax.axis_size(axis))])


def angle_tables(count_rows, count_cols, period):
    left = lax.broadcasted_iota(jnp.int32, (count_rows, count_cols), 0)
    right = lax.broadcasted_iota(jnp.int32, (count_rows, count_cols), 1)
    turns = left * right % period
    angle = turns.astype(jnp.float32) * (2.0 * math.pi / period)
    return (jnp.cos(angle), jnp.sin(angle))


def rotation(cosines, sines, direction):
    upper = jnp.stack([cosines, direction * sines])
    lower_row = jnp.stack([-direction * sines, cosines])
    return jnp.stack([upper, lower_row])


def split_sizes(length):
    period = 2 * length
    first = 1 << (period.bit_length() - 1 + 1) // 2
    return (first, period // first)


def make_tables(first, second):
    cos_first, sin_first = angle_tables(first, first, first)
    cos_twist, sin_twist = angle_tables(first, second, first * second)
    cos_second, sin_second = angle_tables(second, second, second)
    forward_first = rotation(cos_first, sin_first, 1.0)
    inverse_first = rotation(cos_first, sin_first, -1.0)
    forward_second = rotation(cos_second, sin_second, 1.0)
    inverse_second = rotation(cos_second, sin_second, -1.0)
    return (forward_first, inverse_first, forward_second, inverse_second, cos_twist, sin_twist)


def forward_spectrum(signal, tables, first, second):
    forward_first, inverse_first, forward_second, inverse_second, cos_twist, sin_twist = tables
    lower = first // 2
    folded = signal.reshape(2, signal.shape[1], lower, second)
    section = jnp.einsum("brnm,abnk->arkm", folded, forward_first[:, :, :lower], precision=precise)
    turned = jnp.stack(
        [
            section[0] * cos_twist + section[1] * sin_twist,
            section[1] * cos_twist - section[0] * sin_twist,
        ]
    )
    return jnp.einsum("brkm,abmj->arkj", turned, forward_second, precision=precise)


def inverse_spectrum(spectrum, tables, first, second, both):
    forward_first, inverse_first, forward_second, inverse_second, cos_twist, sin_twist = tables
    lower = first // 2
    rows = spectrum.shape[1]
    inner = jnp.einsum("brkj,abjm->arkm", spectrum, inverse_second, precision=precise)
    turned = jnp.stack(
        [inner[0] * cos_twist - inner[1] * sin_twist, inner[1] * cos_twist + inner[0] * sin_twist]
    )
    if both:
        signal = jnp.einsum(
            "brkm,abkn->arnm", turned, inverse_first[:, :, :, :lower], precision=precise
        )
        return (signal / (first * second)).reshape(2, rows, lower * second)
    signal = jnp.einsum("brkm,bkn->rnm", turned, inverse_first[0][:, :, :lower], precision=precise)
    return (signal / (first * second)).reshape(rows, lower * second)


def complex_product(left, right):
    return jnp.stack(
        [left[0] * right[0] - left[1] * right[1], left[0] * right[1] + left[1] * right[0]]
    )


def conjugate_product(left, right):
    return jnp.stack(
        [left[0] * right[0] + left[1] * right[1], left[0] * right[1] - left[1] * right[0]]
    )


def mirror(array, seq_dim):
    moved = array
    for bit_index in range(lax.axis_size("seq").bit_length() - 1):
        moved = swapped(moved, "seq", bit_index)
    return jnp.flip(moved, axis=seq_dim)


def to_channels(stacked):
    return lax.all_to_all(stacked, "seq", split_axis=1, concat_axis=2, tiled=True)


def to_tokens(stacked):
    return lax.all_to_all(stacked, "seq", split_axis=2, concat_axis=1, tiled=True)


def body(tokens, w_query, w_value, w_out, long_filter, cotangent):
    floats = jnp.float32
    halves = jnp.bfloat16
    half = w_query.shape[0]
    seq_count = lax.axis_size("seq")
    batch_count = lax.axis_size("batch")
    length = tokens.shape[1] * seq_count
    first, second = split_sizes(length)
    tables = make_tables(first, second)
    scale = (2.0 * batch_count * length) ** (-0.5)
    source = tokens[0]
    front = source[:, :half]
    back = source[:, half:]
    back_strand = mirror(back, 0)[:, ::-1]
    strands = jnp.stack([front, back_strand])
    query = jnp.einsum("stk,kh->sht", strands, w_query, preferred_element_type=floats).astype(
        halves
    )
    value = jnp.einsum("stk,kh->sht", strands, w_value, preferred_element_type=floats).astype(
        halves
    )
    value_sig = to_channels(value).astype(floats)
    value_spec = forward_spectrum(value_sig, tables, first, second)
    taps_spec = forward_spectrum(
        jnp.stack([long_filter, jnp.zeros_like(long_filter)]), tables, first, second
    )
    conv_sig = inverse_spectrum(complex_product(value_spec, taps_spec), tables, first, second, True)
    conv_tok = to_tokens(conv_sig.astype(halves))
    gated = (query.astype(floats) * conv_tok.astype(floats)).astype(halves)
    gated_back = mirror(gated[1], 1)
    out_front = jnp.einsum("ht,hk->tk", gated[0], w_out, preferred_element_type=floats)
    out_back = jnp.einsum("ht,hk->tk", gated_back, w_out, preferred_element_type=floats)
    block_out = jnp.concatenate(
        [front.astype(floats) + out_front, back.astype(floats) + out_back[:, ::-1]], axis=1
    ).astype(halves)[None]
    upstream = cotangent[0]
    up_front = upstream[:, :half]
    up_back = upstream[:, half:]
    grad_back = mirror(up_back, 0)[:, ::-1]
    grad_strands = jnp.stack([up_front, grad_back])
    grad_gated = jnp.einsum(
        "stk,hk->sht", grad_strands, w_out, preferred_element_type=floats
    ).astype(halves)
    grad_query_t = (grad_gated.astype(floats) * conv_tok.astype(floats)).astype(halves)
    grad_conv = (grad_gated.astype(floats) * query.astype(floats)).astype(halves)
    grad_sig = to_channels(grad_conv).astype(floats)
    grad_spec = forward_spectrum(grad_sig, tables, first, second)
    value_grad_sig = inverse_spectrum(
        conjugate_product(taps_spec, grad_spec), tables, first, second, True
    )
    filter_part = (
        inverse_spectrum(conjugate_product(value_spec, grad_spec), tables, first, second, False)
        * scale
    )
    grad_value_t = to_tokens(value_grad_sig.astype(halves))
    front_in = jnp.einsum(
        "ht,kh->tk", grad_query_t[0], w_query, preferred_element_type=floats
    ) + jnp.einsum("ht,kh->tk", grad_value_t[0], w_value, preferred_element_type=floats)
    paired = jnp.stack([grad_query_t[1], grad_value_t[1]])
    paired = mirror(paired, 2)
    back_in = jnp.einsum(
        "ht,kh->tk", paired[0], w_query, preferred_element_type=floats
    ) + jnp.einsum("ht,kh->tk", paired[1], w_value, preferred_element_type=floats)
    grad_tokens = jnp.concatenate(
        [up_front.astype(floats) + front_in, up_back.astype(floats) + back_in[:, ::-1]], axis=1
    ).astype(halves)[None]
    term_query = jnp.einsum("stk,sht->kh", strands, grad_query_t, preferred_element_type=floats)
    term_value = jnp.einsum("stk,sht->kh", strands, grad_value_t, preferred_element_type=floats)
    term_out = jnp.einsum("sht,stk->hk", gated, grad_strands, preferred_element_type=floats)
    share = lax.psum_scatter(
        jnp.concatenate([term_query, term_value, term_out], axis=1) * scale,
        "seq",
        scatter_dimension=0,
        tiled=True,
    )
    share, filter_total = (
        lax.psum(share.astype(jnp.bfloat16), "batch").astype(jnp.float32),
        lax.psum(filter_part.astype(jnp.bfloat16), "batch").astype(jnp.float32),
    )
    return (
        block_out,
        grad_tokens,
        share[:, :half],
        share[:, half : 2 * half],
        share[:, 2 * half :],
        filter_total,
    )

MESH = pl.DeviceIdType.MESH


def angle_parts(length):
    step = 1 << (length.bit_length() - 1) // 2
    angle = np.pi * (np.arange(length) + 0.5)[None] / length
    coarse = np.arange(length // step)[:, None] * step * angle
    fine = np.arange(step)[:, None] * angle
    return (
        np.stack([np.cos(coarse), np.sin(coarse)]).astype(np.float32),
        np.stack([np.cos(fine), np.sin(fine)]).astype(np.float32),
    )


def matmul(left, right):
    return jnp.dot(left, right, preferred_element_type=jnp.float32)


def matmul_t(left, right):
    return lax.dot_general(
        left, right, (((1,), (1,)), ((), ())), preferred_element_type=jnp.float32
    )


def times(x, h, conj):
    size = x.shape[1] // 2
    xr, xs, hr, hs = x[:, :size], x[:, size:], h[:, :size], h[:, size:]
    if conj:
        return xr * hr + xs * hs, xs * hr - xr * hs
    return xr * hr - xs * hs, xr * hs + xs * hr


def fused(
    peers, scale,
    tok, wq, wv, wo, taps, cot, coarse, fine,
    block, grad_tok, grad_w, grad_f,
    table, strands, ups, strands_t, query, gates, send1, recv1, send2, recv2,
    vspec, gspec, hspec, yspec,
    ssem1, rsem1, lsem1, ssem2, rsem2, lsem2,
):
    f32, b16 = jnp.float32, jnp.bfloat16
    me = lax.axis_index("seq")
    here, half = tok.shape[0], wq.shape[0]
    own = half // peers
    length = here * peers

    barrier = pltpu.get_barrier_semaphore()
    for r in range(1, peers):
        pl.semaphore_signal(
            barrier, inc=1, device_id={"seq": lax.rem(me + r, peers)}, device_id_type=MESH
        )
    flip = (
        lax.broadcasted_iota(jnp.int32, (half, half), 0)
        + lax.broadcasted_iota(jnp.int32, (half, half), 1)
        == half - 1
    ).astype(f32).astype(b16)
    strands[:here] = tok[:, :half]
    strands[here:] = matmul(tok[:, half:], flip).astype(b16)
    value = matmul(strands[...], wv[...]).astype(b16)
    send1[0] = value[:here].T
    send1[1] = value[here:].T
    pl.semaphore_wait(barrier, peers - 1)

    def rows_of(p):
        return pl.ds(pl.multiple_of(p * own, own), own)

    def lanes_of(p):
        return pl.ds(pl.multiple_of(p * here, here), here)

    def out1(part):
        pair = pl.ds(2 * part, 2)
        copies = []
        for r in range(1, peers):
            p = lax.rem(me + r, peers)
            copies.append(
                pltpu.make_async_remote_copy(
                    src_ref=send1.at[pair, rows_of(p), :],
                    dst_ref=recv1.at[pair, :, lanes_of(me)],
                    send_sem=ssem1.at[part, r],
                    recv_sem=rsem1.at[part, r],
                    device_id={"seq": p},
                    device_id_type=MESH,
                )
            )
        copies.append(
            pltpu.make_async_copy(
                send1.at[pair, rows_of(me), :], recv1.at[pair, :, lanes_of(me)], lsem1.at[part]
            )
        )
        for c in copies:
            c.start()
        return copies

    def out2(part):
        pair = pl.ds(2 * part, 2)
        copies = []
        for r in range(1, peers):
            p = lax.rem(me + r, peers)
            copies.append(
                pltpu.make_async_remote_copy(
                    src_ref=send2.at[pair, :, lanes_of(p)],
                    dst_ref=recv2.at[pair, rows_of(me), :],
                    send_sem=ssem2.at[part, r],
                    recv_sem=rsem2.at[part, r],
                    device_id={"seq": p},
                    device_id_type=MESH,
                )
            )
        copies.append(
            pltpu.make_async_copy(
                send2.at[pair, :, lanes_of(me)], recv2.at[pair, rows_of(me), :], lsem2.at[part]
            )
        )
        for c in copies:
            c.start()
        return copies

    first = out1(0)
    ups[:here] = cot[:, :half]
    ups[here:] = matmul(cot[:, half:], flip).astype(b16)
    query[...] = matmul(strands[...], wq[...]).astype(b16)
    gates[...] = matmul_t(ups[...], wo[...]).astype(b16)
    grad_conv = (gates[...].astype(f32) * query[...].astype(f32)).astype(b16)
    send1[2] = grad_conv[:here].T
    send1[3] = grad_conv[here:].T
    second = out1(1)

    count, step = coarse.shape[1], fine.shape[1]

    @pl.loop(0, count)
    def _(a):
        ca, sa = coarse[0, pl.ds(a, 1), :], coarse[1, pl.ds(a, 1), :]
        rows = pl.ds(pl.multiple_of(a * step, step), step)
        table[rows, :length] = (ca * fine[0] - sa * fine[1]).astype(b16)
        table[rows, length:] = (sa * fine[0] + ca * fine[1]).astype(b16)

    strands_t[...] = strands[...].T
    hspec[...] = matmul(taps[...].astype(b16), table[...])

    def spread(part, causal):
        spec = (vspec, gspec)[part]
        for strand in range(2):
            row = pl.ds(strand * own, own)
            r, s = times(spec[row, :], hspec[...], strand != causal)
            yspec[row, :length] = r.astype(b16)
            yspec[row, length:] = s.astype(b16)
        back = (matmul_t(yspec[...], table[...]) * (1.0 / length)).astype(b16)
        send2[2 * part] = back[:own]
        send2[2 * part + 1] = back[own:]

    for c in first:
        c.wait()
    vspec[...] = matmul(recv1[0:2].reshape(2 * own, length), table[...])
    spread(0, 0)
    third = out2(0)
    for c in second:
        c.wait()
    gspec[...] = matmul(recv1[2:4].reshape(2 * own, length), table[...])
    spread(1, 1)
    fourth = out2(1)
    r0, s0 = times(gspec[:own, :], vspec[:own, :], True)
    r1, s1 = times(vspec[own:, :], gspec[own:, :], True)
    yspec[:own, :length] = (r0 + r1).astype(b16)
    yspec[:own, length:] = (s0 + s1).astype(b16)
    grad_f[...] = matmul_t(yspec[:own, :], table[...]) * (scale / length)

    for c in third:
        c.wait()
    conv = jnp.concatenate([recv2[0].T, recv2[1].T], axis=0).astype(f32)
    gated = (query[...].astype(f32) * conv).astype(b16)
    grad_query = (gates[...].astype(f32) * conv).astype(b16)
    grad_w[:, :half] = (matmul(strands_t[...], grad_query) * scale).astype(grad_w.dtype)
    grad_w[:, 2 * half :] = (matmul(gated.T, ups[...]) * scale).astype(grad_w.dtype)
    total = strands[...].astype(f32) + matmul(gated, wo[...])
    block[:, :half] = total[:here].astype(b16)
    block[:, half:] = matmul(total[here:].astype(b16), flip).astype(b16)
    total = ups[...].astype(f32) + matmul_t(grad_query, wq[...])
    for c in fourth:
        c.wait()
    grad_value = jnp.concatenate([recv2[2].T, recv2[3].T], axis=0)
    grad_w[:, half : 2 * half] = (matmul(strands_t[...], grad_value) * scale).astype(grad_w.dtype)
    total = total + matmul_t(grad_value, wv[...])
    grad_tok[:, :half] = total[:here].astype(b16)
    grad_tok[:, half:] = matmul(total[here:].astype(b16), flip).astype(b16)


def short_body(tokens, w_query, w_value, w_out, long_filter, cotangent):
    f32, b16 = jnp.float32, jnp.bfloat16
    half = w_query.shape[0]
    peers = lax.axis_size("seq")
    here = tokens.shape[1]
    length = here * peers
    own = half // peers
    scale = (2.0 * lax.axis_size("batch") * length) ** (-0.5)
    coarse, fine = angle_parts(length)
    dma = pltpu.SemaphoreType.DMA
    block, grad_tok, grad_w, grad_f = pl.pallas_call(
        functools.partial(fused, peers, scale),
        out_shape=(
            jax.ShapeDtypeStruct((here, 2 * half), b16),
            jax.ShapeDtypeStruct((here, 2 * half), b16),
            jax.ShapeDtypeStruct((half, 3 * half), b16),
            jax.ShapeDtypeStruct((own, length), f32),
        ),
        in_specs=[pl.BlockSpec(memory_space=pltpu.VMEM)] * 8,
        out_specs=(pl.BlockSpec(memory_space=pltpu.VMEM),) * 4,
        scratch_shapes=[
            pltpu.VMEM((length, 2 * length), b16),
            pltpu.VMEM((2 * here, half), b16),
            pltpu.VMEM((2 * here, half), b16),
            pltpu.VMEM((half, 2 * here), b16),
            pltpu.VMEM((2 * here, half), b16),
            pltpu.VMEM((2 * here, half), b16),
            pltpu.VMEM((4, half, here), b16),
            pltpu.VMEM((4, own, length), b16),
            pltpu.VMEM((4, own, length), b16),
            pltpu.VMEM((4, half, here), b16),
            pltpu.VMEM((2 * own, 2 * length), f32),
            pltpu.VMEM((2 * own, 2 * length), f32),
            pltpu.VMEM((own, 2 * length), f32),
            pltpu.VMEM((2 * own, 2 * length), b16),
            dma((2, peers)),
            dma((2, peers)),
            dma((2,)),
            dma((2, peers)),
            dma((2, peers)),
            dma((2,)),
        ],
        compiler_params=pltpu.CompilerParams(
            collective_id=0, has_side_effects=True, vmem_limit_bytes=60 << 20
        ),
    )(tokens[0], w_query, w_value, w_out, long_filter, cotangent[0], coarse, fine)
    share = lax.psum_scatter(grad_w, "seq", scatter_dimension=0, tiled=True)
    share = lax.psum(share, "batch").astype(f32)
    total_f = lax.psum(grad_f.astype(b16), "batch").astype(f32)
    return (
        block[None],
        grad_tok[None],
        share[:, :half],
        share[:, half : 2 * half],
        share[:, 2 * half :],
        total_f,
    )


def fits(tokens, peers):
    return (tokens.shape[1] * peers) ** 2 * 4 <= 8 << 20


def choose(tokens, *rest):
    short = fits(tokens, lax.axis_size("seq"))
    return (short_body if short else body)(tokens, *rest)


def solution(mesh):
    in_specs = (P("batch", "seq", None), P(), P(), P(), P("seq", None), P("batch", "seq", None))
    out_specs = (
        P("batch", "seq", None),
        P("batch", "seq", None),
        P("seq", None),
        P("seq", None),
        P("seq", None),
        P("seq", None),
    )
    return jax.shard_map(choose, mesh=mesh, in_specs=in_specs, out_specs=out_specs, check_vma=False)
```

```python
import functools
import math

import jax
import jax.numpy as jnp
import numpy as np
from jax import lax
from jax.experimental import pallas as pl
from jax.experimental.pallas import tpu as pltpu
from jax.sharding import PartitionSpec as P

precise = lax.Precision.HIGH


def swapped(x, axis, stride):
    return lax.ppermute(x, axis, [(i, i ^ 1 << stride) for i in range(lax.axis_size(axis))])


def angle_tables(count_rows, count_cols, period):
    left = lax.broadcasted_iota(jnp.int32, (count_rows, count_cols), 0)
    right = lax.broadcasted_iota(jnp.int32, (count_rows, count_cols), 1)
    turns = left * right % period
    angle = turns.astype(jnp.float32) * (2.0 * math.pi / period)
    return (jnp.cos(angle), jnp.sin(angle))


def rotation(cosines, sines, direction):
    upper = jnp.stack([cosines, direction * sines])
    lower_row = jnp.stack([-direction * sines, cosines])
    return jnp.stack([upper, lower_row])


def split_sizes(length):
    period = 2 * length
    first = 1 << (period.bit_length() - 1 + 1) // 2
    return (first, period // first)


def make_tables(first, second):
    cos_first, sin_first = angle_tables(first, first, first)
    cos_twist, sin_twist = angle_tables(first, second, first * second)
    cos_second, sin_second = angle_tables(second, second, second)
    forward_first = rotation(cos_first, sin_first, 1.0)
    inverse_first = rotation(cos_first, sin_first, -1.0)
    forward_second = rotation(cos_second, sin_second, 1.0)
    inverse_second = rotation(cos_second, sin_second, -1.0)
    return (forward_first, inverse_first, forward_second, inverse_second, cos_twist, sin_twist)


def forward_spectrum(signal, tables, first, second):
    forward_first, inverse_first, forward_second, inverse_second, cos_twist, sin_twist = tables
    lower = first // 2
    folded = signal.reshape(2, signal.shape[1], lower, second)
    section = jnp.einsum("brnm,abnk->arkm", folded, forward_first[:, :, :lower], precision=precise)
    turned = jnp.stack(
        [
            section[0] * cos_twist + section[1] * sin_twist,
            section[1] * cos_twist - section[0] * sin_twist,
        ]
    )
    return jnp.einsum("brkm,abmj->arkj", turned, forward_second, precision=precise)


def inverse_spectrum(spectrum, tables, first, second, both):
    forward_first, inverse_first, forward_second, inverse_second, cos_twist, sin_twist = tables
    lower = first // 2
    rows = spectrum.shape[1]
    inner = jnp.einsum("brkj,abjm->arkm", spectrum, inverse_second, precision=precise)
    turned = jnp.stack(
        [inner[0] * cos_twist - inner[1] * sin_twist, inner[1] * cos_twist + inner[0] * sin_twist]
    )
    if both:
        signal = jnp.einsum(
            "brkm,abkn->arnm", turned, inverse_first[:, :, :, :lower], precision=precise
        )
        return (signal / (first * second)).reshape(2, rows, lower * second)
    signal = jnp.einsum("brkm,bkn->rnm", turned, inverse_first[0][:, :, :lower], precision=precise)
    return (signal / (first * second)).reshape(rows, lower * second)


def complex_product(left, right):
    return jnp.stack(
        [left[0] * right[0] - left[1] * right[1], left[0] * right[1] + left[1] * right[0]]
    )


def conjugate_product(left, right):
    return jnp.stack(
        [left[0] * right[0] + left[1] * right[1], left[0] * right[1] - left[1] * right[0]]
    )


def mirror(array, seq_dim):
    moved = array
    for bit_index in range(lax.axis_size("seq").bit_length() - 1):
        moved = swapped(moved, "seq", bit_index)
    return jnp.flip(moved, axis=seq_dim)


def to_channels(stacked):
    return lax.all_to_all(stacked, "seq", split_axis=1, concat_axis=2, tiled=True)


def to_tokens(stacked):
    return lax.all_to_all(stacked, "seq", split_axis=2, concat_axis=1, tiled=True)


def body(tokens, w_query, w_value, w_out, long_filter, cotangent):
    floats = jnp.float32
    halves = jnp.bfloat16
    half = w_query.shape[0]
    seq_count = lax.axis_size("seq")
    batch_count = lax.axis_size("batch")
    length = tokens.shape[1] * seq_count
    first, second = split_sizes(length)
    tables = make_tables(first, second)
    scale = (2.0 * batch_count * length) ** (-0.5)
    source = tokens[0]
    front = source[:, :half]
    back = source[:, half:]
    back_strand = mirror(back, 0)[:, ::-1]
    strands = jnp.stack([front, back_strand])
    query = jnp.einsum("stk,kh->sht", strands, w_query, preferred_element_type=floats).astype(
        halves
    )
    value = jnp.einsum("stk,kh->sht", strands, w_value, preferred_element_type=floats).astype(
        halves
    )
    value_sig = to_channels(value).astype(floats)
    value_spec = forward_spectrum(value_sig, tables, first, second)
    taps_spec = forward_spectrum(
        jnp.stack([long_filter, jnp.zeros_like(long_filter)]), tables, first, second
    )
    conv_sig = inverse_spectrum(complex_product(value_spec, taps_spec), tables, first, second, True)
    conv_tok = to_tokens(conv_sig.astype(halves))
    gated = (query.astype(floats) * conv_tok.astype(floats)).astype(halves)
    gated_back = mirror(gated[1], 1)
    out_front = jnp.einsum("ht,hk->tk", gated[0], w_out, preferred_element_type=floats)
    out_back = jnp.einsum("ht,hk->tk", gated_back, w_out, preferred_element_type=floats)
    block_out = jnp.concatenate(
        [front.astype(floats) + out_front, back.astype(floats) + out_back[:, ::-1]], axis=1
    ).astype(halves)[None]
    upstream = cotangent[0]
    up_front = upstream[:, :half]
    up_back = upstream[:, half:]
    grad_back = mirror(up_back, 0)[:, ::-1]
    grad_strands = jnp.stack([up_front, grad_back])
    grad_gated = jnp.einsum(
        "stk,hk->sht", grad_strands, w_out, preferred_element_type=floats
    ).astype(halves)
    grad_query_t = (grad_gated.astype(floats) * conv_tok.astype(floats)).astype(halves)
    grad_conv = (grad_gated.astype(floats) * query.astype(floats)).astype(halves)
    grad_sig = to_channels(grad_conv).astype(floats)
    grad_spec = forward_spectrum(grad_sig, tables, first, second)
    value_grad_sig = inverse_spectrum(
        conjugate_product(taps_spec, grad_spec), tables, first, second, True
    )
    filter_part = (
        inverse_spectrum(conjugate_product(value_spec, grad_spec), tables, first, second, False)
        * scale
    )
    grad_value_t = to_tokens(value_grad_sig.astype(halves))
    front_in = jnp.einsum(
        "ht,kh->tk", grad_query_t[0], w_query, preferred_element_type=floats
    ) + jnp.einsum("ht,kh->tk", grad_value_t[0], w_value, preferred_element_type=floats)
    paired = jnp.stack([grad_query_t[1], grad_value_t[1]])
    paired = mirror(paired, 2)
    back_in = jnp.einsum(
        "ht,kh->tk", paired[0], w_query, preferred_element_type=floats
    ) + jnp.einsum("ht,kh->tk", paired[1], w_value, preferred_element_type=floats)
    grad_tokens = jnp.concatenate(
        [up_front.astype(floats) + front_in, up_back.astype(floats) + back_in[:, ::-1]], axis=1
    ).astype(halves)[None]
    term_query = jnp.einsum("stk,sht->kh", strands, grad_query_t, preferred_element_type=floats)
    term_value = jnp.einsum("stk,sht->kh", strands, grad_value_t, preferred_element_type=floats)
    term_out = jnp.einsum("sht,stk->hk", gated, grad_strands, preferred_element_type=floats)
    share = lax.psum_scatter(
        jnp.concatenate([term_query, term_value, term_out], axis=1) * scale,
        "seq",
        scatter_dimension=0,
        tiled=True,
    )
    share, filter_total = (
        lax.psum(share.astype(jnp.bfloat16), "batch").astype(jnp.float32),
        lax.psum(filter_part.astype(jnp.bfloat16), "batch").astype(jnp.float32),
    )
    return (
        block_out,
        grad_tokens,
        share[:, :half],
        share[:, half : 2 * half],
        share[:, 2 * half :],
        filter_total,
    )

MESH = pl.DeviceIdType.MESH


def angle_parts(length):
    step = 1 << (length.bit_length() - 1) // 2
    angle = np.pi * (np.arange(length) + 0.5)[None] / length
    coarse = np.arange(length // step)[:, None] * step * angle
    fine = np.arange(step)[:, None] * angle
    return (
        np.stack([np.cos(coarse), np.sin(coarse)]).astype(np.float32),
        np.stack([np.cos(fine), np.sin(fine)]).astype(np.float32),
    )


def matmul(left, right):
    return jnp.dot(left, right, preferred_element_type=jnp.float32)


def matmul_t(left, right):
    return lax.dot_general(
        left, right, (((1,), (1,)), ((), ())), preferred_element_type=jnp.float32
    )


def times(x, h, conj):
    size = x.shape[1] // 2
    xr, xs, hr, hs = x[:, :size], x[:, size:], h[:, :size], h[:, size:]
    if conj:
        return xr * hr + xs * hs, xs * hr - xr * hs
    return xr * hr - xs * hs, xr * hs + xs * hr


def fused(
    peers, scale,
    tok, wq, wv, wo, taps, cot, coarse, fine,
    block, grad_tok, out_q, out_v, out_o, out_f,
    table, strands, ups, strands_t, query, gates, send1, recv1, send2, recv2,
    vspec, gspec, hspec, yspec,
    ssem1, rsem1, lsem1, ssem2, rsem2, lsem2,
    acc, kept, send_a, recv_a, send_b, recv_b, send_c, recv_c, full,
    acc_f, kept_f, send_af, recv_af, send_bf, recv_bf, full_f,
    ssem_a, rsem_a, ssem_b, rsem_b, ssem_c, rsem_c, ssem_d, rsem_d,
):
    f32, b16 = jnp.float32, jnp.bfloat16
    me = lax.axis_index("seq")
    here, half = tok.shape[0], wq.shape[0]
    own = half // peers
    length = here * peers

    barrier = pltpu.get_barrier_semaphore()
    for r in range(1, peers):
        pl.semaphore_signal(
            barrier, inc=1, device_id={"seq": lax.rem(me + r, peers)}, device_id_type=MESH
        )
    batches = lax.axis_size("batch")
    seat = lax.axis_index("batch")
    for r in range(1, batches):
        pl.semaphore_signal(
            barrier, inc=1, device_id={"batch": lax.rem(seat + r, batches)}, device_id_type=MESH
        )
    low, high = lax.rem(seat, 2), seat // 2
    quarter = own // batches
    slot = 2 * low + high
    flip = (
        lax.broadcasted_iota(jnp.int32, (half, half), 0)
        + lax.broadcasted_iota(jnp.int32, (half, half), 1)
        == half - 1
    ).astype(f32).astype(b16)
    strands[:here] = tok[:, :half]
    strands[here:] = matmul(tok[:, half:], flip).astype(b16)
    value = matmul(strands[...], wv[...]).astype(b16)
    send1[0] = value[:here].T
    send1[1] = value[here:].T
    pl.semaphore_wait(barrier, peers + batches - 2)

    def rows_of(p):
        return pl.ds(pl.multiple_of(p * own, own), own)

    def lanes_of(p):
        return pl.ds(pl.multiple_of(p * here, here), here)

    def out1(part):
        pair = pl.ds(2 * part, 2)
        copies = []
        for r in range(1, peers):
            p = lax.rem(me + r, peers)
            copies.append(
                pltpu.make_async_remote_copy(
                    src_ref=send1.at[pair, rows_of(p), :],
                    dst_ref=recv1.at[pair, :, lanes_of(me)],
                    send_sem=ssem1.at[part, r],
                    recv_sem=rsem1.at[part, r],
                    device_id={"seq": p},
                    device_id_type=MESH,
                )
            )
        copies.append(
            pltpu.make_async_copy(
                send1.at[pair, rows_of(me), :], recv1.at[pair, :, lanes_of(me)], lsem1.at[part]
            )
        )
        for c in copies:
            c.start()
        return copies

    def out2(part):
        pair = pl.ds(2 * part, 2)
        copies = []
        for r in range(1, peers):
            p = lax.rem(me + r, peers)
            copies.append(
                pltpu.make_async_remote_copy(
                    src_ref=send2.at[pair, :, lanes_of(p)],
                    dst_ref=recv2.at[pair, rows_of(me), :],
                    send_sem=ssem2.at[part, r],
                    recv_sem=rsem2.at[part, r],
                    device_id={"seq": p},
                    device_id_type=MESH,
                )
            )
        copies.append(
            pltpu.make_async_copy(
                send2.at[pair, :, lanes_of(me)], recv2.at[pair, rows_of(me), :], lsem2.at[part]
            )
        )
        for c in copies:
            c.start()
        return copies

    def part_of(bit, size):
        return pl.ds(pl.multiple_of(bit * size, size), size)

    def bundle(m):
        if m == 3:
            return acc_f, kept_f, send_af, recv_af, send_bf, recv_bf, full_f
        return (
            acc.at[m], kept.at[m], send_a.at[m], recv_a.at[m], send_b.at[m], recv_b.at[m], full.at[m]
        )

    def swap(src, dst, ssem, rsem, target):
        copy = pltpu.make_async_remote_copy(
            src_ref=src,
            dst_ref=dst,
            send_sem=ssem,
            recv_sem=rsem,
            device_id={"batch": target},
            device_id_type=MESH,
        )
        copy.start()
        return copy

    def stage_a(m):
        total, _, out, into, _, _, _ = bundle(m)
        out[...] = total[:, part_of(1 - low, 2 * quarter), :].astype(b16)
        return swap(out, into, ssem_a.at[m], rsem_a.at[m], 2 * high + 1 - low)

    def stage_b(m, copy):
        total, keep, _, arrived, out, into, _ = bundle(m)
        copy.wait()
        keep[...] = total[:, part_of(low, 2 * quarter), :] + arrived[...].astype(f32)
        out[...] = keep[:, part_of(1 - high, quarter), :].astype(b16)
        return swap(out, into, ssem_b.at[m], rsem_b.at[m], 2 * (1 - high) + low)

    def stage_c(m, copy):
        _, keep, _, _, _, arrived, _ = bundle(m)
        copy.wait()
        mine = (keep[:, part_of(high, quarter), :] + arrived[...].astype(f32)).astype(b16)
        if m == 3:
            full_f[slot] = mine[0]
            return None
        send_c[m] = mine
        copies = []
        for r in range(1, peers):
            p = lax.rem(me + r, peers)
            copies.append(
                pltpu.make_async_remote_copy(
                    src_ref=send_c.at[m, p],
                    dst_ref=recv_c.at[m, me],
                    send_sem=ssem_c.at[m, r],
                    recv_sem=rsem_c.at[m, r],
                    device_id={"seq": p},
                    device_id_type=MESH,
                )
            )
        for c in copies:
            c.start()
        recv_c[m, me] = send_c[m, me]
        return copies

    def stage_d(m, copies):
        whole = bundle(m)[-1]
        if m < 3:
            for c in copies:
                c.wait()
            whole[slot] = jnp.sum(recv_c[m].astype(f32), axis=0).astype(b16)
        return [
            swap(
                whole.at[slot], whole.at[slot], ssem_d.at[m, r], rsem_d.at[m, r],
                lax.rem(seat + r, batches),
            )
            for r in range(1, batches)
        ]

    def finish(m, copies):
        for c in copies:
            c.wait()
        out = (out_q, out_o, out_v, out_f)[m]
        out[...] = bundle(m)[-1][...].astype(f32).reshape(out.shape)

    def weight(m, left, right):
        acc[m] = (matmul(left, right) * scale).reshape(peers, own, half)

    first = out1(0)
    ups[:here] = cot[:, :half]
    ups[here:] = matmul(cot[:, half:], flip).astype(b16)
    query[...] = matmul(strands[...], wq[...]).astype(b16)
    gates[...] = matmul_t(ups[...], wo[...]).astype(b16)
    grad_conv = (gates[...].astype(f32) * query[...].astype(f32)).astype(b16)
    send1[2] = grad_conv[:here].T
    send1[3] = grad_conv[here:].T
    second = out1(1)

    count, step = coarse.shape[1], fine.shape[1]

    @pl.loop(0, count)
    def _(a):
        ca, sa = coarse[0, pl.ds(a, 1), :], coarse[1, pl.ds(a, 1), :]
        rows = pl.ds(pl.multiple_of(a * step, step), step)
        table[rows, :length] = (ca * fine[0] - sa * fine[1]).astype(b16)
        table[rows, length:] = (sa * fine[0] + ca * fine[1]).astype(b16)

    strands_t[...] = strands[...].T
    hspec[...] = matmul(taps[...].astype(b16), table[...])

    def spread(part, causal):
        spec = (vspec, gspec)[part]
        for strand in range(2):
            row = pl.ds(strand * own, own)
            r, s = times(spec[row, :], hspec[...], strand != causal)
            yspec[row, :length] = r.astype(b16)
            yspec[row, length:] = s.astype(b16)
        back = (matmul_t(yspec[...], table[...]) * (1.0 / length)).astype(b16)
        send2[2 * part] = back[:own]
        send2[2 * part + 1] = back[own:]

    for c in first:
        c.wait()
    vspec[...] = matmul(recv1[0:2].reshape(2 * own, length), table[...])
    spread(0, 0)
    third = out2(0)
    for c in second:
        c.wait()
    gspec[...] = matmul(recv1[2:4].reshape(2 * own, length), table[...])
    spread(1, 1)
    fourth = out2(1)
    r0, s0 = times(gspec[:own, :], vspec[:own, :], True)
    r1, s1 = times(vspec[own:, :], gspec[own:, :], True)
    yspec[:own, :length] = (r0 + r1).astype(b16)
    yspec[:own, length:] = (s0 + s1).astype(b16)
    acc_f[0] = matmul_t(yspec[:own, :], table[...]) * (scale / length)
    af = stage_a(3)

    for c in third:
        c.wait()
    conv = jnp.concatenate([recv2[0].T, recv2[1].T], axis=0).astype(f32)
    grad_query = (gates[...].astype(f32) * conv).astype(b16)
    weight(0, strands_t[...], grad_query)
    a0 = stage_a(0)
    gated = (query[...].astype(f32) * conv).astype(b16)
    weight(1, gated.T, ups[...])
    a1 = stage_a(1)
    bf = stage_b(3, af)
    total = strands[...].astype(f32) + matmul(gated, wo[...])
    block[:, :half] = total[:here].astype(b16)
    block[:, half:] = matmul(total[here:].astype(b16), flip).astype(b16)
    b0 = stage_b(0, a0)
    b1 = stage_b(1, a1)
    for c in fourth:
        c.wait()
    grad_value = jnp.concatenate([recv2[2].T, recv2[3].T], axis=0)
    weight(2, strands_t[...], grad_value)
    a2 = stage_a(2)
    c0 = stage_c(0, b0)
    c1 = stage_c(1, b1)
    b2 = stage_b(2, a2)
    stage_c(3, bf)
    df = stage_d(3, None)
    total = ups[...].astype(f32) + matmul_t(grad_query, wq[...]) + matmul_t(grad_value, wv[...])
    grad_tok[:, :half] = total[:here].astype(b16)
    grad_tok[:, half:] = matmul(total[here:].astype(b16), flip).astype(b16)
    c2 = stage_c(2, b2)
    d0 = stage_d(0, c0)
    d1 = stage_d(1, c1)
    d2 = stage_d(2, c2)
    finish(3, df)
    finish(0, d0)
    finish(1, d1)
    finish(2, d2)


def short_body(tokens, w_query, w_value, w_out, long_filter, cotangent):
    f32, b16 = jnp.float32, jnp.bfloat16
    half = w_query.shape[0]
    peers = lax.axis_size("seq")
    here = tokens.shape[1]
    length = here * peers
    own = half // peers
    scale = (2.0 * lax.axis_size("batch") * length) ** (-0.5)
    coarse, fine = angle_parts(length)
    dma = pltpu.SemaphoreType.DMA
    batches = lax.axis_size("batch")
    quarter = own // batches
    vmem = pltpu.VMEM
    block, grad_tok, *sums = pl.pallas_call(
        functools.partial(fused, peers, scale),
        out_shape=(
            jax.ShapeDtypeStruct((here, 2 * half), b16),
            jax.ShapeDtypeStruct((here, 2 * half), b16),
            jax.ShapeDtypeStruct((own, half), f32),
            jax.ShapeDtypeStruct((own, half), f32),
            jax.ShapeDtypeStruct((own, half), f32),
            jax.ShapeDtypeStruct((own, length), f32),
        ),
        in_specs=[pl.BlockSpec(memory_space=pltpu.VMEM)] * 8,
        out_specs=(pl.BlockSpec(memory_space=pltpu.VMEM),) * 6,
        scratch_shapes=[
            pltpu.VMEM((length, 2 * length), b16),
            pltpu.VMEM((2 * here, half), b16),
            pltpu.VMEM((2 * here, half), b16),
            pltpu.VMEM((half, 2 * here), b16),
            pltpu.VMEM((2 * here, half), b16),
            pltpu.VMEM((2 * here, half), b16),
            pltpu.VMEM((4, half, here), b16),
            pltpu.VMEM((4, own, length), b16),
            pltpu.VMEM((4, own, length), b16),
            pltpu.VMEM((4, half, here), b16),
            pltpu.VMEM((2 * own, 2 * length), f32),
            pltpu.VMEM((2 * own, 2 * length), f32),
            pltpu.VMEM((own, 2 * length), f32),
            pltpu.VMEM((2 * own, 2 * length), b16),
            dma((2, peers)),
            dma((2, peers)),
            dma((2,)),
            dma((2, peers)),
            dma((2, peers)),
            dma((2,)),
            vmem((3, peers, own, half), f32),
            vmem((3, peers, 2 * quarter, half), f32),
            vmem((3, peers, 2 * quarter, half), b16),
            vmem((3, peers, 2 * quarter, half), b16),
            vmem((3, peers, quarter, half), b16),
            vmem((3, peers, quarter, half), b16),
            vmem((3, peers, quarter, half), b16),
            vmem((3, peers, quarter, half), b16),
            vmem((3, batches, quarter, half), b16),
            vmem((1, own, length), f32),
            vmem((1, 2 * quarter, length), f32),
            vmem((1, 2 * quarter, length), b16),
            vmem((1, 2 * quarter, length), b16),
            vmem((1, quarter, length), b16),
            vmem((1, quarter, length), b16),
            vmem((batches, quarter, length), b16),
            dma((4,)),
            dma((4,)),
            dma((4,)),
            dma((4,)),
            dma((3, peers)),
            dma((3, peers)),
            dma((4, batches)),
            dma((4, batches)),
        ],
        compiler_params=pltpu.CompilerParams(
            collective_id=0, has_side_effects=True, vmem_limit_bytes=60 << 20
        ),
    )(tokens[0], w_query, w_value, w_out, long_filter, cotangent[0], coarse, fine)
    return (block[None], grad_tok[None], *sums)


def fits(tokens, half):
    peers, batches = lax.axis_size("seq"), lax.axis_size("batch")
    small = (tokens.shape[1] * peers) ** 2 * 4 <= 8 << 20
    return small and batches == 4 and half % (16 * batches * peers) == 0


def choose(tokens, *rest):
    short = fits(tokens, rest[0].shape[0])
    return (short_body if short else body)(tokens, *rest)


def solution(mesh):
    in_specs = (P("batch", "seq", None), P(), P(), P(), P("seq", None), P("batch", "seq", None))
    out_specs = (
        P("batch", "seq", None),
        P("batch", "seq", None),
        P("seq", None),
        P("seq", None),
        P("seq", None),
        P("seq", None),
    )
    return jax.shard_map(choose, mesh=mesh, in_specs=in_specs, out_specs=out_specs, check_vma=False)
```

```python
import functools
import math

import jax
import jax.numpy as jnp
import numpy as np
from jax import lax
from jax.experimental import pallas as pl
from jax.experimental.pallas import tpu as pltpu
from jax.sharding import PartitionSpec as P

precise = lax.Precision.HIGH


def swapped(x, axis, stride):
    return lax.ppermute(x, axis, [(i, i ^ 1 << stride) for i in range(lax.axis_size(axis))])


def angle_tables(count_rows, count_cols, period):
    left = lax.broadcasted_iota(jnp.int32, (count_rows, count_cols), 0)
    right = lax.broadcasted_iota(jnp.int32, (count_rows, count_cols), 1)
    turns = left * right % period
    angle = turns.astype(jnp.float32) * (2.0 * math.pi / period)
    return (jnp.cos(angle), jnp.sin(angle))


def rotation(cosines, sines, direction):
    upper = jnp.stack([cosines, direction * sines])
    lower_row = jnp.stack([-direction * sines, cosines])
    return jnp.stack([upper, lower_row])


def split_sizes(length):
    period = 2 * length
    first = 1 << (period.bit_length() - 1 + 1) // 2
    return (first, period // first)


def make_tables(first, second):
    cos_first, sin_first = angle_tables(first, first, first)
    cos_twist, sin_twist = angle_tables(first, second, first * second)
    cos_second, sin_second = angle_tables(second, second, second)
    forward_first = rotation(cos_first, sin_first, 1.0)
    inverse_first = rotation(cos_first, sin_first, -1.0)
    forward_second = rotation(cos_second, sin_second, 1.0)
    inverse_second = rotation(cos_second, sin_second, -1.0)
    return (forward_first, inverse_first, forward_second, inverse_second, cos_twist, sin_twist)


def forward_spectrum(signal, tables, first, second):
    forward_first, inverse_first, forward_second, inverse_second, cos_twist, sin_twist = tables
    lower = first // 2
    folded = signal.reshape(2, signal.shape[1], lower, second)
    section = jnp.einsum("brnm,abnk->arkm", folded, forward_first[:, :, :lower], precision=precise)
    turned = jnp.stack(
        [
            section[0] * cos_twist + section[1] * sin_twist,
            section[1] * cos_twist - section[0] * sin_twist,
        ]
    )
    return jnp.einsum("brkm,abmj->arkj", turned, forward_second, precision=precise)


def inverse_spectrum(spectrum, tables, first, second, both):
    forward_first, inverse_first, forward_second, inverse_second, cos_twist, sin_twist = tables
    lower = first // 2
    rows = spectrum.shape[1]
    inner = jnp.einsum("brkj,abjm->arkm", spectrum, inverse_second, precision=precise)
    turned = jnp.stack(
        [inner[0] * cos_twist - inner[1] * sin_twist, inner[1] * cos_twist + inner[0] * sin_twist]
    )
    if both:
        signal = jnp.einsum(
            "brkm,abkn->arnm", turned, inverse_first[:, :, :, :lower], precision=precise
        )
        return (signal / (first * second)).reshape(2, rows, lower * second)
    signal = jnp.einsum("brkm,bkn->rnm", turned, inverse_first[0][:, :, :lower], precision=precise)
    return (signal / (first * second)).reshape(rows, lower * second)


def complex_product(left, right):
    return jnp.stack(
        [left[0] * right[0] - left[1] * right[1], left[0] * right[1] + left[1] * right[0]]
    )


def conjugate_product(left, right):
    return jnp.stack(
        [left[0] * right[0] + left[1] * right[1], left[0] * right[1] - left[1] * right[0]]
    )


def mirror(array, seq_dim):
    moved = array
    for bit_index in range(lax.axis_size("seq").bit_length() - 1):
        moved = swapped(moved, "seq", bit_index)
    return jnp.flip(moved, axis=seq_dim)


def to_channels(stacked):
    return lax.all_to_all(stacked, "seq", split_axis=1, concat_axis=2, tiled=True)


def to_tokens(stacked):
    return lax.all_to_all(stacked, "seq", split_axis=2, concat_axis=1, tiled=True)


def body(tokens, w_query, w_value, w_out, long_filter, cotangent):
    floats = jnp.float32
    halves = jnp.bfloat16
    half = w_query.shape[0]
    seq_count = lax.axis_size("seq")
    batch_count = lax.axis_size("batch")
    length = tokens.shape[1] * seq_count
    first, second = split_sizes(length)
    tables = make_tables(first, second)
    scale = (2.0 * batch_count * length) ** (-0.5)
    source = tokens[0]
    front = source[:, :half]
    back = source[:, half:]
    back_strand = mirror(back, 0)[:, ::-1]
    strands = jnp.stack([front, back_strand])
    query = jnp.einsum("stk,kh->sht", strands, w_query, preferred_element_type=floats).astype(
        halves
    )
    value = jnp.einsum("stk,kh->sht", strands, w_value, preferred_element_type=floats).astype(
        halves
    )
    value_sig = to_channels(value).astype(floats)
    value_spec = forward_spectrum(value_sig, tables, first, second)
    taps_spec = forward_spectrum(
        jnp.stack([long_filter, jnp.zeros_like(long_filter)]), tables, first, second
    )
    conv_sig = inverse_spectrum(complex_product(value_spec, taps_spec), tables, first, second, True)
    conv_tok = to_tokens(conv_sig.astype(halves))
    gated = (query.astype(floats) * conv_tok.astype(floats)).astype(halves)
    gated_back = mirror(gated[1], 1)
    out_front = jnp.einsum("ht,hk->tk", gated[0], w_out, preferred_element_type=floats)
    out_back = jnp.einsum("ht,hk->tk", gated_back, w_out, preferred_element_type=floats)
    block_out = jnp.concatenate(
        [front.astype(floats) + out_front, back.astype(floats) + out_back[:, ::-1]], axis=1
    ).astype(halves)[None]
    upstream = cotangent[0]
    up_front = upstream[:, :half]
    up_back = upstream[:, half:]
    grad_back = mirror(up_back, 0)[:, ::-1]
    grad_strands = jnp.stack([up_front, grad_back])
    grad_gated = jnp.einsum(
        "stk,hk->sht", grad_strands, w_out, preferred_element_type=floats
    ).astype(halves)
    grad_query_t = (grad_gated.astype(floats) * conv_tok.astype(floats)).astype(halves)
    grad_conv = (grad_gated.astype(floats) * query.astype(floats)).astype(halves)
    grad_sig = to_channels(grad_conv).astype(floats)
    grad_spec = forward_spectrum(grad_sig, tables, first, second)
    value_grad_sig = inverse_spectrum(
        conjugate_product(taps_spec, grad_spec), tables, first, second, True
    )
    filter_part = (
        inverse_spectrum(conjugate_product(value_spec, grad_spec), tables, first, second, False)
        * scale
    )
    grad_value_t = to_tokens(value_grad_sig.astype(halves))
    front_in = jnp.einsum(
        "ht,kh->tk", grad_query_t[0], w_query, preferred_element_type=floats
    ) + jnp.einsum("ht,kh->tk", grad_value_t[0], w_value, preferred_element_type=floats)
    paired = jnp.stack([grad_query_t[1], grad_value_t[1]])
    paired = mirror(paired, 2)
    back_in = jnp.einsum(
        "ht,kh->tk", paired[0], w_query, preferred_element_type=floats
    ) + jnp.einsum("ht,kh->tk", paired[1], w_value, preferred_element_type=floats)
    grad_tokens = jnp.concatenate(
        [up_front.astype(floats) + front_in, up_back.astype(floats) + back_in[:, ::-1]], axis=1
    ).astype(halves)[None]
    term_query = jnp.einsum("stk,sht->kh", strands, grad_query_t, preferred_element_type=floats)
    term_value = jnp.einsum("stk,sht->kh", strands, grad_value_t, preferred_element_type=floats)
    term_out = jnp.einsum("sht,stk->hk", gated, grad_strands, preferred_element_type=floats)
    share = lax.psum_scatter(
        jnp.concatenate([term_query, term_value, term_out], axis=1) * scale,
        "seq",
        scatter_dimension=0,
        tiled=True,
    )
    share, filter_total = (
        lax.psum(share.astype(jnp.bfloat16), "batch").astype(jnp.float32),
        lax.psum(filter_part.astype(jnp.bfloat16), "batch").astype(jnp.float32),
    )
    return (
        block_out,
        grad_tokens,
        share[:, :half],
        share[:, half : 2 * half],
        share[:, 2 * half :],
        filter_total,
    )

MESH = pl.DeviceIdType.MESH


def angle_parts(length):
    step = 1 << (length.bit_length() - 1) // 2
    angle = np.pi * (np.arange(length) + 0.5)[None] / length
    coarse = np.arange(length // step)[:, None] * step * angle
    fine = np.arange(step)[:, None] * angle
    return (
        np.stack([np.cos(coarse), np.sin(coarse)]).astype(np.float32),
        np.stack([np.cos(fine), np.sin(fine)]).astype(np.float32),
    )


def matmul(left, right):
    return jnp.dot(left, right, preferred_element_type=jnp.float32)


def matmul_t(left, right):
    return lax.dot_general(
        left, right, (((1,), (1,)), ((), ())), preferred_element_type=jnp.float32
    )


def times(x, h, conj):
    size = x.shape[1] // 2
    xr, xs, hr, hs = x[:, :size], x[:, size:], h[:, :size], h[:, size:]
    if conj:
        return xr * hr + xs * hs, xs * hr - xr * hs
    return xr * hr - xs * hs, xr * hs + xs * hr


def fused(
    peers, scale,
    tok_in, wq_in, wv_in, wo_in, taps_in, cot_in, coarse_in, fine_in,
    block_out, grad_out, out_w, out_f,
    block, grad_tok, osem,
    tok, wq, wv, wo, taps, cot, coarse, fine, lsem,
    table, strands, ups, strands_t, query, gates, send1, recv1, send2, recv2,
    vspec, gspec, hspec, yspec,
    ssem1, rsem1, lsem1, ssem2, rsem2, lsem2,
    acc, kept, send_a, recv_a, send_b, recv_b, send_c, recv_c, full,
    acc_f, kept_f, send_af, recv_af, send_bf, recv_bf, full_f,
    ssem_a, rsem_a, ssem_b, rsem_b, ssem_c, rsem_c, ssem_d, rsem_d,
):
    me = lax.axis_index("seq")
    here, half = tok.shape[0], wq.shape[0]
    f32, b16 = jnp.float32, jnp.bfloat16
    own = half // peers
    length = here * peers

    barrier = pltpu.get_barrier_semaphore()
    for r in range(1, peers):
        pl.semaphore_signal(
            barrier, inc=1, device_id={"seq": lax.rem(me + r, peers)}, device_id_type=MESH
        )
    batches = lax.axis_size("batch")
    seat = lax.axis_index("batch")
    for r in range(1, batches):
        pl.semaphore_signal(
            barrier, inc=1, device_id={"batch": lax.rem(seat + r, batches)}, device_id_type=MESH
        )
    loads = {}
    pairs = (
        ("tok", tok_in, tok), ("wv", wv_in, wv), ("cot", cot_in, cot), ("wo", wo_in, wo),
        ("wq", wq_in, wq), ("coarse", coarse_in, coarse), ("fine", fine_in, fine),
        ("taps", taps_in, taps),
    )
    for index, (name, src, dst) in enumerate(pairs):
        loads[name] = pltpu.make_async_copy(src, dst, lsem.at[index])
        loads[name].start()
    low, high = lax.rem(seat, 2), seat // 2
    quarter = own // batches
    slot = 2 * low + high
    flip = (
        lax.broadcasted_iota(jnp.int32, (half, half), 0)
        + lax.broadcasted_iota(jnp.int32, (half, half), 1)
        == half - 1
    ).astype(f32).astype(b16)
    loads["tok"].wait()
    strands[:here] = tok[:, :half]
    strands[here:] = matmul(tok[:, half:], flip).astype(b16)
    loads["wv"].wait()
    value = matmul(strands[...], wv[...]).astype(b16)
    send1[0] = value[:here].T
    send1[1] = value[here:].T
    for name in ("cot", "wo", "wq"):
        loads[name].wait()
    ups[:here] = cot[:, :half]
    ups[here:] = matmul(cot[:, half:], flip).astype(b16)
    query[...] = matmul(strands[...], wq[...]).astype(b16)
    gates[...] = matmul_t(ups[...], wo[...]).astype(b16)
    grad_conv = (gates[...].astype(f32) * query[...].astype(f32)).astype(b16)
    send1[2] = grad_conv[:here].T
    send1[3] = grad_conv[here:].T
    pl.semaphore_wait(barrier, peers + batches - 2)

    def rows_of(p):
        return pl.ds(pl.multiple_of(p * own, own), own)

    def lanes_of(p):
        return pl.ds(pl.multiple_of(p * here, here), here)

    def out1(part):
        pair = pl.ds((0, 2, 3)[part], (2, 1, 1)[part])
        copies = []
        for r in range(1, peers):
            p = lax.rem(me + r, peers)
            copies.append(
                pltpu.make_async_remote_copy(
                    src_ref=send1.at[pair, rows_of(p), :],
                    dst_ref=recv1.at[pair, :, lanes_of(me)],
                    send_sem=ssem1.at[part, r],
                    recv_sem=rsem1.at[part, r],
                    device_id={"seq": p},
                    device_id_type=MESH,
                )
            )
        copies.append(
            pltpu.make_async_copy(
                send1.at[pair, rows_of(me), :], recv1.at[pair, :, lanes_of(me)], lsem1.at[part]
            )
        )
        for c in copies:
            c.start()
        return copies

    def out2(part):
        pair = pl.ds((0, 2, 3)[part], (2, 1, 1)[part])
        copies = []
        for r in range(1, peers):
            p = lax.rem(me + r, peers)
            copies.append(
                pltpu.make_async_remote_copy(
                    src_ref=send2.at[pair, :, lanes_of(p)],
                    dst_ref=recv2.at[pair, rows_of(me), :],
                    send_sem=ssem2.at[part, r],
                    recv_sem=rsem2.at[part, r],
                    device_id={"seq": p},
                    device_id_type=MESH,
                )
            )
        copies.append(
            pltpu.make_async_copy(
                send2.at[pair, :, lanes_of(me)], recv2.at[pair, rows_of(me), :], lsem2.at[part]
            )
        )
        for c in copies:
            c.start()
        return copies

    def part_of(bit, size):
        return pl.ds(pl.multiple_of(bit * size, size), size)

    def bundle(m):
        if m == 3:
            return acc_f, kept_f, send_af, recv_af, send_bf, recv_bf, full_f
        return (
            acc.at[m], kept.at[m], send_a.at[m], recv_a.at[m], send_b.at[m], recv_b.at[m], full.at[m]
        )

    def swap(src, dst, ssem, rsem, target):
        copy = pltpu.make_async_remote_copy(
            src_ref=src,
            dst_ref=dst,
            send_sem=ssem,
            recv_sem=rsem,
            device_id={"batch": target},
            device_id_type=MESH,
        )
        copy.start()
        return copy

    def stage_a(m):
        total, _, out, into, _, _, _ = bundle(m)
        out[...] = total[:, part_of(1 - low, 2 * quarter), :].astype(b16)
        return swap(out, into, ssem_a.at[m], rsem_a.at[m], 2 * high + 1 - low)

    def stage_b(m, copy):
        total, keep, _, arrived, out, into, _ = bundle(m)
        copy.wait()
        keep[...] = total[:, part_of(low, 2 * quarter), :] + arrived[...].astype(f32)
        out[...] = keep[:, part_of(1 - high, quarter), :].astype(b16)
        return swap(out, into, ssem_b.at[m], rsem_b.at[m], 2 * (1 - high) + low)

    def stage_c(m, copy):
        _, keep, _, _, _, arrived, _ = bundle(m)
        copy.wait()
        mine = (keep[:, part_of(high, quarter), :] + arrived[...].astype(f32)).astype(b16)
        if m == 3:
            full_f[slot] = mine[0]
            return None
        send_c[m] = mine
        copies = []
        for r in range(1, peers):
            p = lax.rem(me + r, peers)
            copies.append(
                pltpu.make_async_remote_copy(
                    src_ref=send_c.at[m, p],
                    dst_ref=recv_c.at[m, me],
                    send_sem=ssem_c.at[m, r],
                    recv_sem=rsem_c.at[m, r],
                    device_id={"seq": p},
                    device_id_type=MESH,
                )
            )
        for c in copies:
            c.start()
        recv_c[m, me] = send_c[m, me]
        return copies

    def stage_d(m, copies):
        whole = bundle(m)[-1]
        if m < 3:
            for c in copies:
                c.wait()
            whole[slot] = jnp.sum(recv_c[m].astype(f32), axis=0).astype(b16)
        return [
            swap(
                whole.at[slot], whole.at[slot], ssem_d.at[m, r], rsem_d.at[m, r],
                lax.rem(seat + r, batches),
            )
            for r in range(1, batches)
        ]

    def finish(m, copies):
        for c in copies:
            c.wait()
        target = out_f if m == 3 else out_w.at[m]
        return leave(m, bundle(m)[-1], target)

    def leave(index, src, dst):
        copy = pltpu.make_async_copy(src, dst, osem.at[index])
        copy.start()
        return copy

    def weight(m, left, right):
        acc[m] = (matmul(left, right) * scale).reshape(peers, own, half)

    first = out1(0)
    second = out1(1)
    for name in ("coarse", "fine", "taps"):
        loads[name].wait()

    count, step = coarse.shape[1], fine.shape[1]

    @pl.loop(0, count)
    def _(a):
        ca, sa = coarse[0, pl.ds(a, 1), :], coarse[1, pl.ds(a, 1), :]
        rows = pl.ds(pl.multiple_of(a * step, step), step)
        table[rows, :length] = (ca * fine[0] - sa * fine[1]).astype(b16)
        table[rows, length:] = (sa * fine[0] + ca * fine[1]).astype(b16)

    strands_t[...] = strands[...].T
    hspec[...] = matmul(taps[...].astype(b16), table[...])

    def product(row, spec, conj):
        r, s = times(spec[row, :], hspec[...], conj)
        yspec[row, :length] = r.astype(b16)
        yspec[row, length:] = s.astype(b16)

    def back_value(strand, copies):
        for c in copies:
            c.wait()
        row = pl.ds(strand * own, own)
        gspec[row, :] = matmul(recv1[2 + strand], table[...])
        product(row, gspec, strand == 0)
        send2[2 + strand] = (matmul_t(yspec[row, :], table[...]) * (1.0 / length)).astype(b16)
        return out2(1 + strand)

    for c in first:
        c.wait()
    vspec[...] = matmul(recv1[0:2].reshape(2 * own, length), table[...])
    product(pl.ds(0, own), vspec, False)
    product(pl.ds(own, own), vspec, True)
    conv_own = (matmul_t(yspec[...], table[...]) * (1.0 / length)).astype(b16)
    send2[0] = conv_own[:own]
    send2[1] = conv_own[own:]
    third = out2(0)
    late = out1(2)
    fourth = back_value(0, second)

    for c in third:
        c.wait()
    conv = jnp.concatenate([recv2[0].T, recv2[1].T], axis=0).astype(f32)
    grad_query = (gates[...].astype(f32) * conv).astype(b16)
    weight(0, strands_t[...], grad_query)
    a0 = stage_a(0)
    gated = (query[...].astype(f32) * conv).astype(b16)
    weight(1, gated.T, ups[...])
    a1 = stage_a(1)
    b0 = stage_b(0, a0)
    b1 = stage_b(1, a1)
    fifth = back_value(1, late)
    r0, s0 = times(gspec[:own, :], vspec[:own, :], True)
    r1, s1 = times(vspec[own:, :], gspec[own:, :], True)
    yspec[:own, :length] = (r0 + r1).astype(b16)
    yspec[:own, length:] = (s0 + s1).astype(b16)
    acc_f[0] = matmul_t(yspec[:own, :], table[...]) * (scale / length)
    af = stage_a(3)
    total = strands[...].astype(f32) + matmul(gated, wo[...])
    block[:, :half] = total[:here].astype(b16)
    block[:, half:] = matmul(total[here:].astype(b16), flip).astype(b16)
    o4 = leave(4, block, block_out)
    c0 = stage_c(0, b0)
    bf = stage_b(3, af)
    for c in fourth:
        c.wait()
    value_0 = recv2[2].T
    early = matmul(strands_t[:, :here], value_0)
    c1 = stage_c(1, b1)
    for c in fifth:
        c.wait()
    value_1 = recv2[3].T
    acc[2] = ((early + matmul(strands_t[:, here:], value_1)) * scale).reshape(peers, own, half)
    a2 = stage_a(2)
    stage_c(3, bf)
    b2 = stage_b(2, a2)
    grad_value = jnp.concatenate([value_0, value_1], axis=0)
    total = ups[...].astype(f32) + matmul_t(grad_query, wq[...]) + matmul_t(grad_value, wv[...])
    grad_tok[:, :half] = total[:here].astype(b16)
    grad_tok[:, half:] = matmul(total[here:].astype(b16), flip).astype(b16)
    o5 = leave(5, grad_tok, grad_out)
    c2 = stage_c(2, b2)
    df = stage_d(3, None)
    d0 = stage_d(0, c0)
    d1 = stage_d(1, c1)
    o3 = finish(3, df)
    o0 = finish(0, d0)
    o1 = finish(1, d1)
    d2 = stage_d(2, c2)
    o2 = finish(2, d2)
    for c in (o0, o1, o2, o3, o4, o5):
        c.wait()


def emit(block, grad_tok, weights, filters, block_out, grad_out, out_q, out_v, out_o, out_f):
    block_out[...] = block[...]
    grad_out[...] = grad_tok[...]
    out_q[...] = weights[0].reshape(out_q.shape).astype(out_q.dtype)
    out_o[...] = weights[1].reshape(out_o.shape).astype(out_o.dtype)
    out_v[...] = weights[2].reshape(out_v.shape).astype(out_v.dtype)
    out_f[...] = filters[...].reshape(out_f.shape).astype(out_f.dtype)


def short_body(tokens, w_query, w_value, w_out, long_filter, cotangent):
    f32, b16 = jnp.float32, jnp.bfloat16
    half = w_query.shape[0]
    peers = lax.axis_size("seq")
    here = tokens.shape[1]
    length = here * peers
    own = half // peers
    scale = (2.0 * lax.axis_size("batch") * length) ** (-0.5)
    coarse, fine = angle_parts(length)
    dma = pltpu.SemaphoreType.DMA
    batches = lax.axis_size("batch")
    quarter = own // batches
    vmem = pltpu.VMEM
    arguments = (tokens[0], w_query, w_value, w_out, long_filter, cotangent[0], coarse, fine)
    block, grad_tok, weights, filters = pl.pallas_call(
        functools.partial(fused, peers, scale),
        out_shape=(
            jax.ShapeDtypeStruct((here, 2 * half), b16),
            jax.ShapeDtypeStruct((here, 2 * half), b16),
            jax.ShapeDtypeStruct((3, batches, quarter, half), b16),
            jax.ShapeDtypeStruct((batches, quarter, length), b16),
        ),
        in_specs=[pl.BlockSpec(memory_space=pltpu.HBM)] * 8,
        out_specs=(pl.BlockSpec(memory_space=pltpu.HBM),) * 4,
        scratch_shapes=[
            vmem((here, 2 * half), b16),
            vmem((here, 2 * half), b16),
            dma((6,)),
            *(vmem(a.shape, a.dtype) for a in arguments),
            dma((8,)),
            pltpu.VMEM((length, 2 * length), b16),
            pltpu.VMEM((2 * here, half), b16),
            pltpu.VMEM((2 * here, half), b16),
            pltpu.VMEM((half, 2 * here), b16),
            pltpu.VMEM((2 * here, half), b16),
            pltpu.VMEM((2 * here, half), b16),
            pltpu.VMEM((4, half, here), b16),
            pltpu.VMEM((4, own, length), b16),
            pltpu.VMEM((4, own, length), b16),
            pltpu.VMEM((4, half, here), b16),
            pltpu.VMEM((2 * own, 2 * length), f32),
            pltpu.VMEM((2 * own, 2 * length), f32),
            pltpu.VMEM((own, 2 * length), f32),
            pltpu.VMEM((2 * own, 2 * length), b16),
            dma((3, peers)),
            dma((3, peers)),
            dma((3,)),
            dma((3, peers)),
            dma((3, peers)),
            dma((3,)),
            vmem((3, peers, own, half), f32),
            vmem((3, peers, 2 * quarter, half), f32),
            vmem((3, peers, 2 * quarter, half), b16),
            vmem((3, peers, 2 * quarter, half), b16),
            vmem((3, peers, quarter, half), b16),
            vmem((3, peers, quarter, half), b16),
            vmem((3, peers, quarter, half), b16),
            vmem((3, peers, quarter, half), b16),
            vmem((3, batches, quarter, half), b16),
            vmem((1, own, length), f32),
            vmem((1, 2 * quarter, length), f32),
            vmem((1, 2 * quarter, length), b16),
            vmem((1, 2 * quarter, length), b16),
            vmem((1, quarter, length), b16),
            vmem((1, quarter, length), b16),
            vmem((batches, quarter, length), b16),
            dma((4,)),
            dma((4,)),
            dma((4,)),
            dma((4,)),
            dma((3, peers)),
            dma((3, peers)),
            dma((4, batches)),
            dma((4, batches)),
        ],
        compiler_params=pltpu.CompilerParams(
            collective_id=0, has_side_effects=True, vmem_limit_bytes=65900000
        ),
    )(*arguments)
    block, grad_tok, *sums = pl.pallas_call(
        emit,
        out_shape=(
            jax.ShapeDtypeStruct((here, 2 * half), b16),
            jax.ShapeDtypeStruct((here, 2 * half), b16),
            jax.ShapeDtypeStruct((own, half), f32),
            jax.ShapeDtypeStruct((own, half), f32),
            jax.ShapeDtypeStruct((own, half), f32),
            jax.ShapeDtypeStruct((own, length), f32),
        ),
        in_specs=[pl.BlockSpec(memory_space=pltpu.VMEM)] * 4,
        out_specs=(pl.BlockSpec(memory_space=pltpu.VMEM),) * 6,
        compiler_params=pltpu.CompilerParams(vmem_limit_bytes=65900000),
    )(block, grad_tok, weights, filters)
    return (block[None], grad_tok[None], *sums)


def fits(tokens, half):
    peers, batches = lax.axis_size("seq"), lax.axis_size("batch")
    small = (tokens.shape[1] * peers) ** 2 * 4 <= 8 << 20
    return small and batches == 4 and half % (16 * batches * peers) == 0


def choose(tokens, *rest):
    short = fits(tokens, rest[0].shape[0])
    return (short_body if short else body)(tokens, *rest)


def solution(mesh):
    in_specs = (P("batch", "seq", None), P(), P(), P(), P("seq", None), P("batch", "seq", None))
    out_specs = (
        P("batch", "seq", None),
        P("batch", "seq", None),
        P("seq", None),
        P("seq", None),
        P("seq", None),
        P("seq", None),
    )
    return jax.shard_map(choose, mesh=mesh, in_specs=in_specs, out_specs=out_specs, check_vma=False)
```
